32 devices in a mesh: dp: 8 (over z, core), head: 4 (over y, x).
Axes of the slice: x: 2, y: 2, z: 4, core: 2. Of those that a mesh axis runs over, the one named last changes fastest.
Arguments:
- queries: bfloat16 [1024, 12288], P('dp', 'head'), may hold values from -120 to 120
- latent: bfloat16 [1024, 512], P('dp'), may hold values from -6 to 6
- key_rope: bfloat16 [1024, 64], P('dp'), may hold values from -6 to 6
- kv_gain: bfloat16 [512], replicated, may hold values from 0.099609375 to 1.8984375
- w_kv: bfloat16 [512, 12288], P(None, 'head'), may hold values from -0.25 to 0.25
- grad_out: bfloat16 [1024, 4096], P('dp', 'head'), may hold values from -6 to 6
- positions: int32 [1024], replicated, may hold values from 0 to 1023, as said below
Outputs:
- d_queries: bfloat16 [1024, 12288], P('dp', 'head')
- d_latent: bfloat16 [1024, 512], P('dp', 'head')
- d_key_rope: bfloat16 [1024, 64], P('dp')
- d_gain: float32 [512], P('head')
- d_w_kv: bfloat16 [512, 12288], P('dp', 'head')
The draws below stay inside these ranges and needn't reach their ends.
Inputs may be any that keep to these rules, and one draw needn't show every extreme that they name: `positions`: every position 0 to 1023 appears exactly once.
All inputs are finite; a program needn't handle non-finite values.
Results may differ from the reference program's by a relative error of at most 0.012.
The reference program's roundings to bfloat16 on the way count: a program that leaves them out, or rounds other values in their place, can miss the bound.
Values may be sent and summed in bfloat16 or wider, within the bound.
No kernel may reach another device: no remote copies, remote signals or barrier semaphores. Data moves between devices by JAX's collectives and lax.ppermute only.
A program may use at most 128 MiB of HBM per device.

```python
import math
import jax
import jax.numpy as jnp
from jax import lax

HEADS = 64
KV_LAT = 512
NOPE = 128
ROPE = 64
VDIM = 64
TOK_DEV = 128
TOKENS = 1024
LENGTH = 1024


def paired_draw(key):
    base = jax.random.fold_in(key, 7)
    key_one, key_two = jax.random.split(base, 2)
    rope_keys = jnp.clip(jax.random.normal(key_one, (TOKENS, ROPE), jnp.float32), -6.0, 6.0)
    query_values = jnp.clip(jax.random.normal(key_two, (TOKENS, HEADS, NOPE + ROPE), jnp.float32), -6.0, 6.0)
    return (query_values.reshape(TOKENS, HEADS * (NOPE + ROPE)), rope_keys)


def draw_queries(key, part):
    query_values, rope_keys = paired_draw(key)
    return query_values.astype(jnp.bfloat16)


def draw_key_rope(key, part):
    query_values, rope_keys = paired_draw(key)
    return rope_keys.astype(jnp.bfloat16)


def draw_positions(key, part):
    order = jax.random.permutation(jax.random.fold_in(key, 11), LENGTH)
    return order.astype(jnp.int32)


def block_levels(own_key, extent, shards, smallest, largest):
    loudness = 1.0
    for axis_at, shards_of in shards:
        heights = jax.random.uniform(jax.random.fold_in(jax.random.fold_in(own_key, 6), axis_at), (shards_of,), jnp.float32, smallest / len(shards), largest / len(shards))
        loudness = loudness * jnp.repeat(jnp.exp(heights), extent[axis_at] // shards_of).reshape((-1,) + (1,) * (len(extent) - 1 - axis_at))
    return loudness


def noise(rng, extent, scale, most, pieces=(), held_as=jnp.bfloat16):
    values = scale * jax.random.normal(rng, extent, jnp.float32)
    if pieces:
        values = values * block_levels(rng, extent, pieces, -0.22, 0.18)
    return jnp.clip(values, -most, most).astype(held_as)


def setup_inputs(seed: int = 0) -> dict:
    splits = jax.random.split(jax.random.key(seed), 8)
    return {
        "queries": draw_queries(jax.random.fold_in(splits[7], 71), 0),
        "latent": noise(splits[1], (TOKENS, KV_LAT), 1.0, 6.0, ((0, 8),)),
        "key_rope": draw_key_rope(jax.random.fold_in(splits[7], 71), 0),
        "kv_gain": jnp.clip(1.0 + 0.18 * jax.random.normal(splits[3], (KV_LAT,), jnp.float32), 0.099609375, 1.8984375).astype(jnp.bfloat16),
        "w_kv": noise(splits[4], (KV_LAT, HEADS * (NOPE + VDIM)), KV_LAT ** -0.5, 0.25, ((1, 4),)),
        "grad_out": noise(splits[5], (TOKENS, HEADS * VDIM), 1.0, 6.0, ((0, 8), (1, 4))),
        "positions": draw_positions(jax.random.fold_in(splits[7], 71), 0),
    }


def rotate(values, places):
    half_width = values.shape[-1] // 2
    frequency = 10000.0 ** (-jnp.arange(half_width, dtype=jnp.float32) / half_width)
    angles = places.astype(jnp.float32)[:, None] * frequency[None, :]
    angles = angles.reshape((values.shape[0],) + (1,) * (values.ndim - 2) + (half_width,))
    cosine = jnp.cos(angles)
    sines = jnp.sin(angles)
    leading = values[..., :half_width]
    trailing = values[..., half_width:]
    return jnp.concatenate([leading * cosine - trailing * sines, trailing * cosine + leading * sines], -1)

def reference(queries, latent, key_rope, kv_gain, w_kv, grad_out, positions):
    query_width = NOPE + ROPE
    pair_width = NOPE + VDIM
    score_scale = 1.0 / math.sqrt(query_width)
    groups = TOKENS // TOK_DEV
    latent_wide = latent.astype(jnp.float32)
    root_mean = jnp.sqrt(lax.optimization_barrier(jnp.mean(latent_wide * latent_wide, -1, keepdims=True)) + 1e-06)
    normed = latent_wide / root_mean
    gain_wide = kv_gain.astype(jnp.float32)
    latent_low = (normed * gain_wide).astype(jnp.bfloat16)
    kv_rows = jnp.dot(latent_low, w_kv, preferred_element_type=jnp.float32).astype(jnp.bfloat16)
    kv_rows = kv_rows.reshape(TOKENS, HEADS, pair_width)
    keys_turned = rotate(key_rope.astype(jnp.float32), positions).astype(jnp.bfloat16)
    query_heads = queries.reshape(TOKENS, HEADS, query_width)
    query_turned = rotate(query_heads[..., NOPE:].astype(jnp.float32), positions).astype(jnp.bfloat16)
    query_full = jnp.concatenate([query_heads[..., :NOPE], query_turned], -1)
    grads_heads = grad_out.reshape(TOKENS, HEADS, VDIM)
    visible = positions[None, :] <= positions[:, None]

    def one_head(head_pack):
        query_head, kv_head, grads_head = head_pack
        key_full = jnp.concatenate([kv_head[:, :NOPE], keys_turned], -1)
        value_head = kv_head[:, NOPE:]
        scores = jnp.dot(query_head, key_full.T, preferred_element_type=jnp.float32) * score_scale
        masked = jnp.where(visible, scores, -jnp.inf)
        row_peak = lax.optimization_barrier(jnp.max(masked, -1, keepdims=True))
        row_total = lax.optimization_barrier(jnp.sum(jnp.exp(masked - row_peak), -1, keepdims=True))
        attention = jnp.exp(masked - (row_peak + jnp.log(row_total)))
        attention_low = attention.astype(jnp.bfloat16)
        attended = jnp.dot(attention_low, value_head, preferred_element_type=jnp.float32)
        row_delta = lax.optimization_barrier(jnp.sum(grads_head.astype(jnp.float32) * attended, -1, keepdims=True))
        dprobs = jnp.dot(grads_head, value_head.T, preferred_element_type=jnp.float32)
        dscores = (attention * (dprobs - row_delta) * score_scale).astype(jnp.bfloat16)
        grad_query = jnp.dot(dscores, key_full, preferred_element_type=jnp.float32)
        score_groups = dscores.astype(jnp.float32).reshape(groups, TOK_DEV, TOKENS)
        query_groups = query_head[:, :NOPE].astype(jnp.float32).reshape(groups, TOK_DEV, NOPE)
        key_parts = jnp.einsum('gij,gid->gjd', score_groups, query_groups)
        weight_groups = attention_low.astype(jnp.float32).reshape(groups, TOK_DEV, TOKENS)
        output_groups = grads_head.astype(jnp.float32).reshape(groups, TOK_DEV, VDIM)
        value_parts = jnp.einsum('gij,gid->gjd', weight_groups, output_groups)
        pair_parts = jnp.concatenate([key_parts, value_parts], -1).astype(jnp.bfloat16)
        pair_parts = lax.optimization_barrier(pair_parts)
        pair_sum = lax.optimization_barrier(jnp.sum(pair_parts.astype(jnp.float32), 0))
        rope_grad = jnp.dot(dscores.T, query_head[:, NOPE:], preferred_element_type=jnp.float32)
        return (grad_query, pair_sum, rope_grad)
    grad_query, grad_pairs, grad_turned = lax.map(one_head, (query_full.swapaxes(0, 1), kv_rows.swapaxes(0, 1), grads_heads.swapaxes(0, 1)))
    grad_query = grad_query.swapaxes(0, 1)
    grad_pairs = grad_pairs.swapaxes(0, 1)
    rope_grads = lax.optimization_barrier(jnp.sum(grad_turned, 0))
    query_back = rotate(grad_query[..., NOPE:], -positions)
    d_queries = jnp.concatenate([grad_query[..., :NOPE], query_back], -1).reshape(TOKENS, -1).astype(jnp.bfloat16)
    kv_grads = grad_pairs.reshape(TOKENS, HEADS * pair_width)
    latent_grads = jnp.dot(kv_grads, w_kv.astype(jnp.float32).T, precision=lax.Precision.HIGHEST)
    d_key_rope = rotate(rope_grads, -positions).astype(jnp.bfloat16)
    weight_total = jnp.dot(latent_low.astype(jnp.float32).T, kv_grads, precision=lax.Precision.HIGHEST)
    d_w_kv = weight_total.astype(jnp.bfloat16)
    scaled = latent_grads * gain_wide
    row_mean = lax.optimization_barrier(jnp.mean(scaled * normed, -1, keepdims=True))
    d_latent = ((scaled - normed * row_mean) / root_mean).astype(jnp.bfloat16)
    d_gain = lax.optimization_barrier(jnp.sum(latent_grads * normed, 0))
    return (d_queries, d_latent, d_key_rope, d_gain, d_w_kv)
```

```python
import math

import jax
import jax.numpy as jnp
from jax import lax
from jax.experimental import pallas as pl
from jax.experimental.pallas import tpu as pltpu
from jax.sharding import PartitionSpec as P

NOPE = 128
ROPE = 64
VDIM = 64
QW = NOPE + ROPE
PW = NOPE + VDIM
KEY_BLOCK = 256
F32 = jnp.float32
BF16 = jnp.bfloat16


def swap(value, axis, mask):
    count = lax.axis_size(axis)
    return lax.ppermute(value, axis, [(i, i ^ mask) for i in range(count)])


def dot(a, b, ca, cb):
    return lax.dot_general(a, b, (((ca,), (cb,)), ((), ())), preferred_element_type=F32)


def turn(x, cosine, sines):
    half = x.shape[-1] // 2
    return x * cosine + jnp.concatenate([x[:, half:], x[:, :half]], -1) * sines


def prep_kernel(latent_ref, rope_ref, gain_ref, cos_ref, sin_ref, block_ref):
    wide = latent_ref[...].astype(F32)
    root = jnp.sqrt(jnp.mean(wide * wide, -1, keepdims=True) + 1e-06)
    low = wide / root * gain_ref[...].astype(F32)
    turned = turn(rope_ref[...].astype(F32), cos_ref[...], sin_ref[...])
    block_ref[...] = jnp.concatenate([low.astype(BF16), turned.astype(BF16)], -1)


def pair_kernel(first, last, core_ref, rows_ref, posk_ref, posq_ref, qa_ref, qb_ref, ga_ref, gb_ref,
                w_ref, cos_ref, sin_ref, *rest):
    if first:
        acc_in = rope_in = None
    else:
        acc_in, rope_in, *rest = rest
    dqa_ref, dqb_ref, dw_ref, acc_out, rope_out, *rest = rest
    if last:
        send_ref, ext_ref, *rest = rest
    kv_ref, s_ref, d_ref, p_ref, g_ref = rest
    total = rows_ref.shape[0]
    lat_width = w_ref.shape[0]
    blocks = total // KEY_BLOCK
    scale = 1.0 / math.sqrt(QW)

    def each(body, init):
        if blocks <= 4:
            for b in range(blocks):
                init = body(pl.ds(b * KEY_BLOCK, KEY_BLOCK), init)
            return init
        return lax.fori_loop(
            0, blocks, lambda b, c: body(pl.ds(pl.multiple_of(b * KEY_BLOCK, KEY_BLOCK), KEY_BLOCK), c), init
        )

    def project(at, carry):
        kv_ref[at, :] = dot(rows_ref[at, :lat_width], w_ref[...], 1, 0).astype(BF16)
        return carry

    each(project, 0)
    q_pair = jnp.concatenate([qa_ref[...], qb_ref[...]], 0)
    g_pair = jnp.concatenate([ga_ref[...], gb_ref[...]], 0)
    queries = q_pair.shape[0]
    dq_parts = []
    for h in range(2):
        q = q_pair[:, h * QW:(h + 1) * QW]
        spin = turn(q[:, NOPE:].astype(F32), cos_ref[...], sin_ref[...]).astype(BF16)
        q = jnp.concatenate([q[:, :NOPE], spin], -1)
        g = g_pair[:, h * VDIM:(h + 1) * VDIM]

        def keys_at(at):
            plain = kv_ref[at, h * PW:h * PW + NOPE]
            return jnp.concatenate([plain, rows_ref[at, lat_width:]], -1)

        def scores(at, peak):
            s = dot(keys_at(at), q, 1, 1) * scale
            s = jnp.where(posk_ref[at, :] <= posq_ref[...], s, -1e30)
            s_ref[at, :] = s
            return jnp.maximum(peak, jnp.max(s, 0, keepdims=True))

        peak = each(scores, jnp.full((1, queries), -1e30, F32))

        def expo(at, total_sum):
            e = jnp.exp(s_ref[at, :] - peak)
            s_ref[at, :] = e
            return total_sum + jnp.sum(e, 0, keepdims=True)

        inverse = 1.0 / each(expo, jnp.zeros((1, queries), F32))

        def deltas(at, delta):
            probs = s_ref[at, :] * inverse
            s_ref[at, :] = probs
            low = probs.astype(BF16)
            p_ref[at, :] = low
            values = kv_ref[at, h * PW + NOPE:(h + 1) * PW]
            dp = dot(values, g, 1, 1)
            d_ref[at, :] = dp
            return delta + jnp.sum(low.astype(F32) * dp, 0, keepdims=True)

        delta = each(deltas, jnp.zeros((1, queries), F32))

        def grads(at, dq):
            ds = (s_ref[at, :] * (d_ref[at, :] - delta) * scale).astype(BF16)
            dk = dot(ds, q, 1, 0)
            dv = dot(p_ref[at, :], g, 1, 0)
            g_ref[at, h * PW:h * PW + NOPE] = dk[:, :NOPE].astype(BF16)
            g_ref[at, h * PW + NOPE:(h + 1) * PW] = dv.astype(BF16)
            spin_part = dk[:, NOPE:]
            if h == 0:
                rope_out[at, :] = spin_part if first else rope_in[at, :] + spin_part
            else:
                rope_out[at, :] = rope_out[at, :] + spin_part
            return dq + dot(ds, keys_at(at), 0, 0)

        dq = each(grads, jnp.zeros((queries, QW), F32))
        back = turn(dq[:, NOPE:], cos_ref[...], -sin_ref[...])
        dq_parts += [dq[:, :NOPE].astype(BF16), back.astype(BF16)]
    dq_pair = jnp.concatenate(dq_parts, -1)
    dqa_ref[...] = dq_pair[:queries // 2]
    dqb_ref[...] = dq_pair[queries // 2:]

    def weights(at, carry):
        return carry + dot(rows_ref[at, :lat_width], g_ref[at, :], 0, 0)

    dw_ref[...] = each(weights, jnp.zeros(dw_ref.shape, F32)).astype(BF16)

    def latents(at, gain_sum):
        part = dot(g_ref[at, :], w_ref[...], 1, 1)
        if not first:
            part = acc_in[at, :] + part
        acc_out[at, :] = part
        if last:
            product = part * rows_ref[at, :lat_width].astype(F32)
            row_sum = jnp.sum(product, -1, keepdims=True)
            ext_ref[at, :ROPE] = rope_out[at, :]
            ext_ref[at, ROPE:] = jnp.broadcast_to(row_sum, (KEY_BLOCK, ROPE))
            gain_sum = gain_sum + jnp.sum(product, 0, keepdims=True)
        return gain_sum

    gain_sum = each(latents, jnp.zeros((1, lat_width), F32))
    if last:
        send_ref[...] = jnp.broadcast_to(gain_sum, send_ref.shape)


def whole(shape):
    return pl.BlockSpec(shape, lambda i, c: (0,) * len(shape))


def run_pair(index, pairs, core, rows, posk, posq, qa, qb, ga, gb, w, cosines, sines, acc, rope):
    first, last = index == 0, index == pairs - 1
    total, width = rows.shape
    lat_width = w.shape[0]
    tokens = qa.shape[0]
    queries = 2 * tokens
    own = lambda i, c: (0, c[0] * pairs + index)
    other = lambda i, c: (0, index)
    in_specs = [
        whole((total, width)),
        whole((total, 1)),
        whole((1, queries)),
        pl.BlockSpec((tokens, 2 * QW), own),
        pl.BlockSpec((tokens, 2 * QW), other),
        pl.BlockSpec((tokens, 2 * VDIM), own),
        pl.BlockSpec((tokens, 2 * VDIM), other),
        pl.BlockSpec((lat_width, 2 * PW), own),
        whole((queries, ROPE)),
        whole((queries, ROPE)),
    ]
    operands = [rows, posk, posq, qa, qb, ga, gb, w, cosines, sines]
    if not first:
        in_specs += [whole((total, lat_width)), whole((total, ROPE))]
        operands += [acc, rope]
    out_shape = [
        jax.ShapeDtypeStruct((tokens, 2 * QW), BF16),
        jax.ShapeDtypeStruct((tokens, 2 * QW), BF16),
        jax.ShapeDtypeStruct((lat_width, 2 * PW), BF16),
        jax.ShapeDtypeStruct((total, lat_width), F32),
        jax.ShapeDtypeStruct((total, ROPE), F32),
    ]
    if last:
        out_shape += [
            jax.ShapeDtypeStruct((8, lat_width), F32),
            jax.ShapeDtypeStruct((total, 2 * ROPE), F32),
        ]
    return pl.pallas_call(
        lambda *refs: pair_kernel(first, last, *refs),
        name=f"pair_{index}",
        out_shape=out_shape,
        grid_spec=pltpu.PrefetchScalarGridSpec(
            num_scalar_prefetch=1,
            grid=(1,),
            in_specs=in_specs,
            out_specs=[whole(o.shape) for o in out_shape],
            scratch_shapes=[
                pltpu.VMEM((total, 2 * PW), BF16),
                pltpu.VMEM((total, queries), F32),
                pltpu.VMEM((total, queries), F32),
                pltpu.VMEM((total, queries), BF16),
                pltpu.VMEM((total, 2 * PW), BF16),
            ],
        ),
        compiler_params=pltpu.CompilerParams(vmem_limit_bytes=60 * 1024 * 1024),
    )(core, *operands)


def body(queries, latent, key_rope, kv_gain, w_kv, grad_out, positions):
    tokens = queries.shape[0]
    lat_width = latent.shape[1]
    members = lax.axis_size("dp")
    heads = lax.axis_size("head")
    depth = members // 2
    my_index = lax.axis_index("dp")
    my_head = lax.axis_index("head")
    core = my_index % 2
    half_q = queries.shape[1] // 2
    half_g = grad_out.shape[1] // 2
    pairs = half_q // (2 * QW)

    def places_of(index):
        return lax.dynamic_slice_in_dim(positions, index * tokens, tokens)

    own_places = places_of(my_index)
    q_places = jnp.concatenate([own_places, places_of(my_index ^ 1)])
    frequency = 10000.0 ** (-jnp.arange(ROPE // 2, dtype=F32) / (ROPE // 2))
    angles = q_places.astype(F32)[:, None] * frequency[None, :]
    cosine, sine = jnp.cos(angles), jnp.sin(angles)
    cosines = jnp.concatenate([cosine, cosine], -1)
    sines = jnp.concatenate([-sine, sine], -1)
    gain_row = kv_gain[None, :]
    block = pl.pallas_call(
        prep_kernel, name="prep", out_shape=jax.ShapeDtypeStruct((tokens, lat_width + ROPE), BF16)
    )(latent, key_rope, gain_row, cosines[:tokens], sines[:tokens])

    away = lambda x, half: lax.dynamic_slice_in_dim(x, (1 - core) * half, half, 1)
    q_other = swap(away(queries, half_q), "dp", 1)
    g_other = swap(away(grad_out, half_g), "dp", 1)

    mine = jnp.concatenate([block] + [swap(block, "dp", 2 * s) for s in range(1, depth)], 0)
    rows = jnp.concatenate([mine, swap(mine, "dp", 1)], 0)
    key_places = jnp.concatenate(
        [places_of(my_index ^ (2 * s + k)) for k in range(2) for s in range(depth)]
    )
    core_arg = core.astype(jnp.int32)[None]
    acc = rope = None
    dq_own, dq_back, dw_parts = [], [], []
    share = lat_width // depth
    z_place = my_index // 2
    for index in range(pairs):
        dqa, dqb, dw, acc, rope, *extra = run_pair(
            index, pairs, core_arg, rows, key_places[:, None], q_places[None, :], queries, q_other,
            grad_out, g_other, w_kv, cosines, sines, acc, rope,
        )
        dq_own.append(dqa)
        dq_back.append(swap(dqb, "dp", 1))
        dw_blocks = dw.reshape(depth, share, dw.shape[1])
        take = lambda s: lax.dynamic_index_in_dim(dw_blocks, z_place ^ s, 0, keepdims=False)
        got = take(0).astype(F32)
        for s in range(1, depth):
            got = got + swap(take(s), "dp", 2 * s).astype(F32)
        dw_parts.append(got.astype(BF16))
    gain_part, ext = extra

    half_rows = tokens * depth
    pad = jnp.zeros((8, 2 * ROPE), F32)
    send = jnp.concatenate([acc[half_rows:], gain_part], 0).astype(BF16)
    sum_lat = jnp.concatenate([acc[:half_rows], gain_part], 0) + swap(send, "dp", 1).astype(F32)
    sum_ext = ext[:half_rows] + swap(ext[half_rows:].astype(BF16), "dp", 1).astype(F32)
    columns = lat_width // heads
    low_lat = sum_lat.astype(BF16)
    low_ext = jnp.concatenate([sum_ext, pad], 0).astype(BF16)

    def cols(x, s):
        return lax.dynamic_slice_in_dim(x, (my_head ^ s) * columns, columns, 1)

    tally = jnp.concatenate([cols(sum_lat, 0), jnp.concatenate([sum_ext, pad], 0)], -1)
    for s in range(1, heads):
        tally = tally + swap(jnp.concatenate([cols(low_lat, s), low_ext], -1), "head", s).astype(F32)
    low = tally.astype(BF16)
    gain_low = low[half_rows:]
    final = jnp.concatenate([tally[:tokens], tally[half_rows:]], 0)
    for s in range(1, depth):
        message = jnp.concatenate([low[s * tokens:(s + 1) * tokens], gain_low], 0)
        final = final + swap(message, "dp", 2 * s).astype(F32)

    wide = latent.astype(F32)
    root = jnp.sqrt(jnp.mean(wide * wide, -1, keepdims=True) + 1e-06)
    normed_cols = cols(wide, 0) / root
    gain_cols = lax.dynamic_slice_in_dim(kv_gain, my_head * columns, columns).astype(F32)
    row_mean = final[:tokens, columns + ROPE:columns + ROPE + 1] / lat_width
    d_latent = ((final[:tokens, :columns] * gain_cols - normed_cols * row_mean) / root).astype(BF16)
    d_gain = final[tokens, :columns] / gain_cols
    rope_grads = final[:tokens, columns:columns + ROPE]
    d_key_rope = turn(rope_grads, cosines[:tokens], -sines[:tokens]).astype(BF16)

    lead = core == 0

    def join(own, other):
        own = jnp.concatenate(own, -1)
        other = jnp.concatenate(other, -1)
        return jnp.concatenate([jnp.where(lead, own, other), jnp.where(lead, other, own)], -1)

    d_queries = join(dq_own, dq_back)
    rows_out = share // 2
    half_of = lambda x, k: lax.dynamic_slice_in_dim(x, k * rows_out, rows_out, 0)
    d_w_kv = join(
        [half_of(part, core) for part in dw_parts],
        [swap(half_of(part, 1 - core), "dp", 1) for part in dw_parts],
    )
    return (d_queries, d_latent, d_key_rope, d_gain, d_w_kv)


def solution(mesh):
    return jax.shard_map(
        body,
        mesh=mesh,
        in_specs=(
            P("dp", "head"),
            P("dp", None),
            P("dp", None),
            P(),
            P(None, "head"),
            P("dp", "head"),
            P(),
        ),
        out_specs=(P("dp", "head"), P("dp", "head"), P("dp", None), P("head"), P("dp", "head")),
        check_vma=False,
    )
```
